32 devices in a mesh: mp: 2 (over y), survey: 16 (over z, x, core).
Axes of the slice: x: 2, y: 2, z: 4, core: 2. Of those that a mesh axis runs over, the one named last changes fastest.
Arguments:
- model: bfloat16 [64, 64, 128], P(('mp', 'survey')), may hold values from -6 to 6
- observed: bfloat16 [32, 64, 128], P(('mp', 'survey')), may hold values from -6 to 6
- weights: bfloat16 [32, 64, 128], P(('mp', 'survey')), may hold values from 0.29882812 to 3
- sensitivity: bfloat16 [2, 2048, 128, 128], P('mp', 'survey'), may hold values from -0.046875 to 0.046875
- block_rows: int32 [2, 2048], P('mp', 'survey'), may hold values from 0 to 15
- block_cols: int32 [2, 2048], P('mp', 'survey'), may hold values from 0 to 3
- block_count: int32 [2, 16], P('mp', 'survey'), may hold values from 32 to 128, as said below
Outputs:
- gradient: float32 [64, 64, 128], P(('mp', 'survey'))
The draws below stay inside these ranges and needn't reach their ends.
Inputs may be any that keep to these rules, and one draw needn't show every extreme that they name: `block_count`: some device uses all 128 slots.
All inputs are finite; a program needn't handle non-finite values.
Results may differ from the reference program's by a relative error of at most 0.0017.
Values may be sent and summed in bfloat16 or wider, within the bound.
A program may use at most 64 MiB of HBM per device.

```python
import math
import jax
import jax.numpy as jnp
from jax import lax

B = 128
NT = 64
KB = 128
MB_DEV = 2
DB_DEV = 1
DB = 16
SL = 4
NMB = 64
NDB = 32
N_MP = 2
N_SURVEY = 16


def draw_block_count(key, part):
    counts = jax.random.randint(key, (N_MP, N_SURVEY), KB // 4, KB + 1)
    spot = jax.random.randint(jax.random.fold_in(key, 7), (), 0, N_MP * N_SURVEY)
    flat_counts = counts.reshape(-1).at[spot].set(KB)
    return flat_counts.reshape(N_MP, N_SURVEY).astype(jnp.int32)


def touch_ends(entries, own_key, smallest, high):
    extent = entries.shape
    index_at = [jax.random.randint(jax.random.fold_in(own_key, axis), (), 0, extent[axis]) for axis in range(len(extent))]
    entries = entries.at[tuple(index_at)].set(smallest)
    longest = extent.index(max(extent))
    index_at[longest] = (index_at[longest] + 1) % extent[longest]
    return entries.at[tuple(index_at)].set(high)


def steps_of(stream_key, extent, pieces, least, largest):
    loudness, own = 1.0, jax.random.fold_in(stream_key, 6)
    for dim, shards_of in pieces:
        steps = jnp.exp(jax.random.uniform(jax.random.fold_in(own, dim), (shards_of,), jnp.float32, least / len(pieces), largest / len(pieces)))
        loudness = loudness * jnp.repeat(steps, extent[dim] // shards_of).reshape([-1 if axis == dim else 1 for axis in range(len(extent))])
    return loudness


def scatter_about(stream_key, extent, deviation, bound, cuts=(), kind=jnp.bfloat16):
    factor_of = steps_of(stream_key, extent, cuts, -0.22, 0.18) if cuts else 1.0
    drawn = jax.random.normal(stream_key, extent, jnp.float32) * deviation * factor_of
    return jnp.minimum(jnp.maximum(drawn, -bound), bound).astype(kind)


def setup_inputs(seed: int = 0) -> dict:
    keys = jax.random.split(jax.random.key(seed), 8)
    return {
        "model": scatter_about(keys[0], (NMB, NT, B), 1.0, 6.0, ((0, 32),)),
        "observed": scatter_about(keys[1], (NDB, NT, B), 1.0, 6.0, ((0, 32),)),
        "weights": jnp.clip(jnp.exp(math.log(3.0) - 2.306499 * jax.random.uniform(keys[2], (NDB, NT, B), jnp.float32) ** steps_of(keys[2], (NDB, NT, B), ((0, 32),), -0.2, 0.2)), 0.29882812, 3.0).astype(jnp.bfloat16),
        "sensitivity": scatter_about(keys[3], (N_MP, N_SURVEY * KB, B, B), (KB * B) ** -0.5, 0.046875, ((0, 2), (1, 16))),
        "block_rows": touch_ends(jax.random.randint(keys[4], (N_MP, N_SURVEY * KB), 0, DB), jax.random.fold_in(keys[4], 1), 0, DB - 1).astype(jnp.int32),
        "block_cols": touch_ends(jax.random.randint(keys[5], (N_MP, N_SURVEY * KB), 0, SL), jax.random.fold_in(keys[5], 1), 0, SL - 1).astype(jnp.int32),
        "block_count": draw_block_count(jax.random.fold_in(keys[7], 71), 0),
    }


SMOOTH = 0.5


def smoothing(model):
    field_f32 = model.astype(jnp.float32)
    earlier = jnp.concatenate([field_f32[:, :1], field_f32[:, :-1]], axis=1)
    later_step = jnp.concatenate([field_f32[:, 1:], field_f32[:, -1:]], axis=1)
    return SMOOTH * (2.0 * field_f32 - earlier - later_step)


def reference(model, observed, weights, sensitivity, block_rows, block_cols, block_count):
    group_rows = DB_DEV * N_SURVEY
    slab_rows = MB_DEV * N_MP
    slabs = jnp.transpose(model.reshape(N_MP, N_SURVEY, MB_DEV, NT, B), (1, 0, 2, 3, 4)).reshape(N_SURVEY, slab_rows, NT, B)
    in_use_all = jnp.arange(KB, dtype=jnp.int32)[None, None, :] < block_count[:, :, None]
    row_ids_all = block_rows.reshape(N_MP, N_SURVEY, KB)
    col_ids_all = block_cols.reshape(N_MP, N_SURVEY, KB)
    blocks_all = sensitivity.reshape(N_MP, N_SURVEY, KB, B, B)
    seen_all = observed.reshape(N_MP, group_rows, NT, B)
    weight_all = weights.reshape(N_MP, group_rows, NT, B)
    survey_ids = jnp.arange(N_SURVEY, dtype=jnp.int32)[:, None]

    def one_group(running, group_item):
        blocks, row_ids, col_ids, in_use, seen_data, data_weight = group_item
        picked = slabs[survey_ids, col_ids]
        terms = jnp.einsum('sktc,skrc->sktr', picked.astype(jnp.float32), blocks.astype(jnp.float32))
        terms = jnp.where(in_use[:, :, None, None], terms, 0.0)
        predicted = jax.ops.segment_sum(terms.reshape(N_SURVEY * KB, NT, B), row_ids.reshape(-1), num_segments=group_rows)
        residual = (data_weight.astype(jnp.float32) * (predicted - seen_data.astype(jnp.float32))).astype(jnp.bfloat16)
        resid_rows = residual[row_ids]
        back_terms = jnp.einsum('sktr,skrc->sktc', resid_rows.astype(jnp.float32), blocks.astype(jnp.float32))
        back_terms = jnp.where(in_use[:, :, None, None], back_terms, 0.0)
        flat_ids = (survey_ids * slab_rows + col_ids).reshape(-1).astype(jnp.int32)
        gradient_slab = jax.ops.segment_sum(back_terms.reshape(N_SURVEY * KB, NT, B), flat_ids, num_segments=N_SURVEY * slab_rows)
        return running + gradient_slab.reshape(N_SURVEY, slab_rows, NT, B), None

    start_sum = jnp.zeros((N_SURVEY, slab_rows, NT, B), jnp.float32)
    summed, _ = lax.scan(one_group, start_sum, (blocks_all, row_ids_all, col_ids_all, in_use_all, seen_all, weight_all))
    misfit_gradient = jnp.transpose(summed.reshape(N_SURVEY, N_MP, MB_DEV, NT, B), (1, 0, 2, 3, 4)).reshape(N_MP * N_SURVEY * MB_DEV, NT, B)
    return misfit_gradient + smoothing(model)
```

```python
import functools

import jax
import jax.numpy as jnp
from jax import lax
from jax.experimental import pallas as pl
from jax.experimental.pallas import tpu as pltpu
from jax.sharding import PartitionSpec as P

SMOOTH = 0.5
MESH = pl.DeviceIdType.MESH
PARTS = 8
GROUPS = 2
FLIPS = 8
SWAPS = 2
LIMIT = 40
PLACES = 256
FULL = 32000.0
FINE = 256.0
TINY = 1e-30


def smoothing(field):
    steps = field.shape[0]
    at = lax.broadcasted_iota(jnp.int32, field.shape, 0)
    earlier = jnp.where(at == 0, field, pltpu.roll(field, 1, 0))
    later_step = jnp.where(at == steps - 1, field, pltpu.roll(field, steps - 1, 0))
    return SMOOTH * (2.0 * field - earlier - later_step)


def pair_tables(ids, tall, labels, count):
    slots = ids.shape[1]
    wide = jnp.broadcast_to(ids, (slots, slots))
    j = lax.broadcasted_iota(jnp.int32, (slots, slots), 0)
    q = lax.broadcasted_iota(jnp.int32, (slots, slots), 1)
    ones = lambda mask, axis: jnp.sum(jnp.where(mask, 1, 0), axis=axis, keepdims=True)
    same = wide == tall
    rank = ones(same & (q < j), 1)
    rank_wide = ones(same & (j < q), 0)
    opens = (rank_wide % 2 == 0) & (q[:1] < count)
    start = ones((wide < tall) & opens, 1)
    used = j[:, :1] < count
    place = jnp.where(used, 2 * start + rank, -1)
    at = lax.broadcasted_iota(jnp.int32, (slots, PLACES), 1)
    hit = place == at
    pick = lambda value: jnp.sum(jnp.where(hit, value, 0), axis=0, keepdims=True)
    slot = pick(j[:, :1] - slots) + slots
    label = pick(labels[:, :1])
    before = pick(jnp.where(rank > 0, 1, 0)) * (at[:1] // 2)
    done = ones((tall <= q) & used & (rank % 2 == 0), 0)
    last = jnp.where(ones((tall == q) & used, 0) > 0, done, 0)
    last = jnp.concatenate([last] * (PLACES // slots), axis=1)
    return slot, label, before, last


SLOT, LABEL, BEFORE, LAST = range(4)


def encode(value):
    rows, cells = value.shape
    tiles = value.reshape(rows // 8, 8, cells)
    top = jnp.maximum(jnp.max(jnp.abs(tiles), axis=0), TINY)
    code = jnp.ceil(jnp.log2(top) * FINE)
    whole = jnp.round(tiles * (FULL * jnp.exp2(code * (-1.0 / FINE)))).reshape(rows, cells)
    code = jnp.concatenate([code, code], axis=0)
    return jnp.concatenate([whole, code], axis=0).astype(jnp.int32).astype(jnp.int16)


def decode(sent):
    rows, cells = sent.shape
    wide = sent.astype(jnp.int32).astype(jnp.float32)
    scale = jnp.exp2(wide[rows - 8:] * (1.0 / FINE)) * (1.0 / FULL)
    return (wide[: rows - 16].reshape(rows // 8 - 2, 8, cells) * scale).reshape(rows - 16, cells)


def copy(src, dst, sems, j, device):
    return pltpu.make_async_remote_copy(
        src_ref=src,
        dst_ref=dst,
        send_sem=sems.at[0, j],
        recv_sem=sems.at[1, j],
        device_id=device,
        device_id_type=MESH,
    )


def collect(
    n_mp, n_survey, per, rows_hbm, cols_hbm, count_hbm, model_hbm, sens_hbm,
    table, slab, blocks, turned, ids_ref, count_ref, tables, load_sem, small_sem, model_sem,
):
    m = lax.axis_index("mp")
    s = lax.axis_index("survey")
    chips = n_survey // 2
    slots = sens_hbm.shape[1]
    owned = model_hbm.shape[0]
    here = pl.ds(m * owned, owned)
    barrier = pltpu.get_barrier_semaphore()
    for j in range(1, n_mp):
        pl.semaphore_signal(
            barrier, inc=1, device_id=((m + j) % n_mp, s), device_id_type=MESH
        )
    smalls = [
        pltpu.make_async_copy(count_hbm, count_ref, small_sem.at[0]),
        pltpu.make_async_copy(rows_hbm, ids_ref.at[0], small_sem.at[1]),
        pltpu.make_async_copy(cols_hbm, ids_ref.at[1], small_sem.at[2]),
        pltpu.make_async_copy(model_hbm, slab.at[here], small_sem.at[3]),
    ]
    part = slots // PARTS
    loads = [
        pltpu.make_async_copy(
            sens_hbm.at[0, pl.ds(i * part, part)], blocks.at[pl.ds(i * part, part)], load_sem.at[i]
        )
        for i in range(PARTS)
    ]
    for load in smalls + loads:
        load.start()
    blocks[slots] = jnp.zeros(blocks.shape[1:], blocks.dtype)
    turned[slots] = jnp.zeros(turned.shape[1:], turned.dtype)
    for small in smalls[:3]:
        small.wait()
    count = count_ref[0, 0]
    owner = ids_ref[0] // per
    rows = (owner % 2 * chips + owner // 2) * per + ids_ref[0] % per
    cols = ids_ref[1]
    tall = lambda ids: jnp.broadcast_to(ids, (slots, slots)).T
    rows_tall, cols_tall = tall(rows), tall(cols)
    made = pair_tables(rows, rows_tall, cols_tall, count)
    made += pair_tables(cols, cols_tall, rows_tall, count)
    for i, one in enumerate(made):
        tables[pl.ds(i, 1)] = one
    to_scalars = pltpu.make_async_copy(tables, table, small_sem.at[4])
    to_scalars.start()
    if n_mp > 1:
        pl.semaphore_wait(barrier, n_mp - 1)
    sends = [
        copy(model_hbm, slab.at[here], model_sem, j - 1, ((m + j) % n_mp, s))
        for j in range(1, n_mp)
    ]
    for send in sends:
        send.start()
    for i, load in enumerate(loads):
        load.wait()

        def turn(g, carry):
            for u in range(FLIPS):
                slot = i * part + g * FLIPS + u
                turned[slot] = blocks[slot].T
            return carry

        lax.fori_loop(0, part // FLIPS, turn, 0)
    for load in [to_scalars, smalls[3]]:
        load.wait()
    for send in sends:
        send.wait()


def kernel(
    n_mp, n_survey, table, slab, blocks, turned, model_ref, seen_ref, weight_ref, out_ref,
    chain, sib_send, sib_recv, chip_send, chip_recv, resid, grad_send, grad_recv,
    sib_sem, chip_sem, gather_sem, relay_sem, grad_sem,
):
    m = lax.axis_index("mp")
    s = lax.axis_index("survey")
    chips = n_survey // 2
    chip, core = s // 2, s % 2
    sibling = (m, chip * 2 + 1 - core)
    slots = blocks.shape[0] - 1
    steps, cells = model_ref.shape[1:]
    owned = model_ref.shape[0]
    per = seen_ref.shape[0]

    def chip_at(j):
        return chip ^ j

    barrier = pltpu.get_barrier_semaphore()
    partners = [((m + j) % n_mp, s) for j in range(1, n_mp)] + [sibling]
    partners += [(m, chip_at(j) * 2 + core) for j in range(1, chips)]
    for partner in partners:
        pl.semaphore_signal(barrier, inc=1, device_id=partner, device_id_type=MESH)
    for i in range(owned):
        out_ref[i] = smoothing(model_ref[i].astype(jnp.float32))
    chain[0] = jnp.zeros(chain.shape[1:], jnp.float32)

    def sums(ids, base, rows, mats):
        pairs = (slots + ids) // 2
        unroll = pairs // GROUPS

        def body(g, carry):
            first = g * unroll
            terms = []
            for u in range(unroll):
                a, b = 2 * (first + u), 2 * (first + u) + 1
                left = [rows[table[base + LABEL, a]], rows[table[base + LABEL, b]]]
                right = [mats[table[base + SLOT, a]], mats[table[base + SLOT, b]]]
                terms.append(
                    jnp.dot(
                        jnp.concatenate(left, axis=1),
                        jnp.concatenate(right, axis=0),
                        preferred_element_type=jnp.float32,
                    )
                )
            for u in range(unroll):
                before = chain[table[base + BEFORE, 2 * (first + u)]]
                chain[first + u + 1] = terms[u] + before
            return carry

        lax.fori_loop(0, GROUPS, body, 0)

    sums(per * n_survey, 0, slab, turned)
    pl.semaphore_wait(barrier, len(partners))

    order = list(range(chips - 1, -1, -1))
    group = chips // SWAPS
    swaps, scatters, gathers, returns = {}, {}, {}, {}
    for p, j in enumerate(order):
        for i in range(per):
            row = ((1 - core) * chips + chip_at(j)) * per + i
            sib_send[p, i] = chain[table[LAST, row]]
        if (p + 1) % group == 0:
            some = pl.ds(p + 1 - group, group)
            swaps[p] = copy(sib_send.at[some], sib_recv.at[some], sib_sem, p, sibling)
            swaps[p].start()
    for p, j in enumerate(order):
        if p % group == 0:
            swaps[p + group - 1].wait_recv()
        mine = []
        for i in range(per):
            row = (core * chips + chip_at(j)) * per + i
            mine.append(chain[table[LAST, row]] + sib_recv[p, i])
        mine = mine[0] if per == 1 else jnp.concatenate(mine, axis=0)
        if j:
            chip_send[j] = encode(mine)
            scatters[j] = copy(
                chip_send.at[j], chip_recv.at[j], chip_sem, j, (m, chip_at(j) * 2 + core)
            )
            scatters[j].start()

    total = mine
    for j in range(1, chips):
        scatters[j].wait_recv()
        total += decode(chip_recv[j])
    total = total.reshape(per, steps, cells)
    value = weight_ref[...].astype(jnp.float32) * (total - seen_ref[...].astype(jnp.float32))
    here = pl.ds((core * chips + chip) * per, per)
    resid[here] = value.astype(jnp.bfloat16)
    for j in order[:-1]:
        gathers[j] = copy(
            resid.at[here], resid.at[here], gather_sem, j, (m, chip_at(j) * 2 + core)
        )
        gathers[j].start()
    half = chips // 2
    relays = []
    for k in range(2):
        for j in range(k * half, (k + 1) * half):
            if j:
                gathers[j].wait_recv()
        some = resid.at[pl.ds((core * chips + (chip // half ^ k) * half) * per, half * per)]
        relays.append(copy(some, some, relay_sem, k, sibling))
        relays[k].start()
    for relay in relays:
        relay.wait_recv()

    sums(owned * n_mp, 4, resid, blocks)

    for j in range(1, n_mp):
        owner = (m + j) % n_mp
        for i in range(owned):
            grad_send[j, i] = chain[table[4 + LAST, owner * owned + i]]
        returns[j] = copy(grad_send.at[j], grad_recv.at[j], grad_sem, j, (owner, s))
        returns[j].start()
    for i in range(owned):
        out_ref[i] += chain[table[4 + LAST, m * owned + i]]
    for j in range(1, n_mp):
        returns[j].wait_recv()
        out_ref[...] += grad_recv[j]

    for relay in relays:
        relay.wait_send()
    for sent in (swaps, scatters, gathers, returns):
        for one in sent.values():
            one.wait_send()


def on_device(
    n_mp, n_survey, model, observed, weights, sensitivity, block_rows, block_cols, block_count
):
    slots = block_rows.shape[1]
    owned, steps, cells = model.shape
    per = observed.shape[0]
    chips = n_survey // 2
    pair = lambda n: pltpu.SemaphoreType.DMA((2, n))
    f32, bf16, i32 = jnp.float32, jnp.bfloat16, jnp.int32
    hbm = pl.BlockSpec(memory_space=pl.ANY)
    smem = pl.BlockSpec(memory_space=pltpu.SMEM)
    vmem = pl.BlockSpec(memory_space=pltpu.VMEM)
    keep = lambda x: pltpu.with_memory_space_constraint(x, pltpu.HBM)
    share = pltpu.VMEM((chips, per, steps, cells), f32)
    coded = pltpu.VMEM((chips, per * steps + 16, cells), jnp.int16)
    pairs = (slots + max(per * n_survey, owned * n_mp)) // 2
    table, slab, blocks, turned = pl.pallas_call(
        functools.partial(collect, n_mp, n_survey, per),
        out_shape=[
            jax.ShapeDtypeStruct((8, PLACES), i32),
            jax.ShapeDtypeStruct((owned * n_mp, steps, cells), bf16),
            jax.ShapeDtypeStruct((slots + 1, cells, cells), bf16),
            jax.ShapeDtypeStruct((slots + 1, cells, cells), bf16),
        ],
        in_specs=[hbm, hbm, pl.BlockSpec(memory_space=pltpu.HBM), hbm, hbm],
        out_specs=[smem, vmem, vmem, vmem],
        scratch_shapes=[
            pltpu.VMEM((2, 1, slots), i32),
            pltpu.SMEM((1, 1), i32),
            pltpu.VMEM((8, PLACES), i32),
            pltpu.SemaphoreType.DMA((PARTS,)),
            pltpu.SemaphoreType.DMA((5,)),
            pair(n_mp),
        ],
        compiler_params=pltpu.CompilerParams(
            collective_id=0, has_side_effects=True, vmem_limit_bytes=LIMIT << 20
        ),
    )(keep(block_rows), keep(block_cols), block_count, keep(model), keep(sensitivity))
    return pl.pallas_call(
        functools.partial(kernel, n_mp, n_survey),
        out_shape=jax.ShapeDtypeStruct(model.shape, f32),
        in_specs=[smem] + [vmem] * 6,
        out_specs=vmem,
        scratch_shapes=[
            pltpu.VMEM((pairs + 1, steps, cells), f32),
            share,
            share,
            coded,
            coded,
            pltpu.VMEM((per * n_survey, steps, cells), bf16),
            pltpu.VMEM((n_mp, owned, steps, cells), f32),
            pltpu.VMEM((n_mp, owned, steps, cells), f32),
            pair(chips),
            pair(chips),
            pair(chips),
            pair(chips),
            pair(n_mp),
        ],
        compiler_params=pltpu.CompilerParams(
            collective_id=1, has_side_effects=True, vmem_limit_bytes=LIMIT << 20
        ),
    )(table, slab, blocks, turned, model, observed, weights)


def solution(mesh):
    n_mp, n_survey = mesh.shape["mp"], mesh.shape["survey"]
    in_specs = (
        P(("mp", "survey"), None, None),
        P(("mp", "survey"), None, None),
        P(("mp", "survey"), None, None),
        P("mp", "survey", None, None),
        P("mp", "survey"),
        P("mp", "survey"),
        P("mp", "survey"),
    )
    out_specs = P(("mp", "survey"), None, None)
    return jax.shard_map(
        functools.partial(on_device, n_mp, n_survey),
        mesh=mesh,
        in_specs=in_specs,
        out_specs=out_specs,
        check_vma=False,
    )
```
